256 devices in a mesh: stn: 16 (over y, x_hi, core), tm: 16 (over z, x_lo).
Axes of the slice: x: 4 (x_hi: 2, x_lo: 2; x = x_hi * 2 + x_lo), y: 4, z: 8, core: 2. Of those that a mesh axis runs over, the one named last changes fastest.
Arguments:
- signal: bfloat16 [32, 4096, 256], P('stn', 'tm'), may hold values from -8 to 8
- cotangent: bfloat16 [32, 4096, 256], P('stn', 'tm'), may hold values from -6 to 6
- window_query: bfloat16 [256, 256], replicated, as said below
- window_key: bfloat16 [256, 256], replicated, as said below
- window_value: bfloat16 [256, 256], replicated, may hold values from -0.375 to 0.375
- window_out: bfloat16 [256, 256], replicated, may hold values from -0.375 to 0.375
- station_query: bfloat16 [256, 256], replicated, as said below
- station_key: bfloat16 [256, 256], replicated, as said below
- station_value: bfloat16 [256, 256], replicated, may hold values from -0.375 to 0.375
- station_out: bfloat16 [256, 256], replicated, may hold values from -0.375 to 0.375
- neighbours: int32 [32, 16], replicated, may hold values from 0 to 31
- neighbour_valid: int32 [32, 16], replicated, may hold values 0 or 1
Outputs:
- block_output: bfloat16 [32, 4096, 256], P('stn', 'tm')
- signal_grad: bfloat16 [32, 4096, 256], P('stn', 'tm')
- grad_window_query: float32 [256, 256], replicated
- grad_window_key: float32 [256, 256], replicated
- grad_window_value: float32 [256, 256], replicated
- grad_window_out: float32 [256, 256], replicated
- grad_station_query: float32 [256, 256], replicated
- grad_station_key: float32 [256, 256], replicated
- grad_station_value: float32 [256, 256], replicated
- grad_station_out: float32 [256, 256], replicated
The draws below stay inside these ranges and needn't reach their ends.
Inputs may be any that keep to these rules, and one draw needn't show every extreme that they name: `window_query`: a projection scaled by its fan-in. `window_key`: a projection scaled by its fan-in. `station_query`: a projection scaled by its fan-in. `station_key`: a projection scaled by its fan-in.
All inputs are finite; a program needn't handle non-finite values.
Results may differ from the reference program's by a relative error of at most 0.015.
The reference program's roundings to bfloat16 on the way count: a program that leaves them out, or rounds other values in their place, can miss the bound.
Values may be sent and summed in bfloat16 or wider, within the bound.
A program may use at most 64 MiB of HBM per device.

```python
import math
import jax
import jax.numpy as jnp
from jax import lax

D = 256
HEADS = 4
NBR = 16
HALF = 128
FR_DEV = 256
STATIONS = 32
FRAMES = 4096
FR_STN = 16


def draw_signal(key, part):
    inner = jax.random.fold_in(key, 5)
    values = jax.random.normal(inner, (STATIONS, FRAMES, D), jnp.float32)
    return jnp.clip(values, -4.0, 4.0).astype(jnp.bfloat16)


def paired_weights(key, salt):
    inner = jax.random.fold_in(key, salt)
    first_key = jax.random.fold_in(inner, 1)
    second_key = jax.random.fold_in(inner, 2)
    spread = 1.0 / math.sqrt(D)
    queried = jnp.clip(jax.random.normal(first_key, (D, D), jnp.float32), -4.0, 4.0) * spread
    keyed_rows = jnp.clip(jax.random.normal(second_key, (D, D), jnp.float32), -4.0, 4.0) * spread
    return (queried, keyed_rows)


def draw_window_query(key, part):
    return paired_weights(key, 11)[0].astype(jnp.bfloat16)


def draw_window_key(key, part):
    return paired_weights(key, 11)[1].astype(jnp.bfloat16)


def draw_station_query(key, part):
    return paired_weights(key, 12)[0].astype(jnp.bfloat16)


def draw_station_key(key, part):
    return paired_weights(key, 12)[1].astype(jnp.bfloat16)


def set_ends(entries, key, low, top_value):
    longest = entries.shape.index(max(entries.shape))
    spots = []
    for shift in (0, 1):
        where = [jax.random.randint(jax.random.fold_in(key, axis), (), 0, length) for axis, length in enumerate(entries.shape)]
        where[longest] = (where[longest] + shift) % entries.shape[longest]
        spots.append(tuple(where))
    return entries.at[spots[0]].set(low).at[spots[1]].set(top_value)


def level_of(rng, shape, split, least, largest):
    def one(dim, parts):
        heights = jax.random.uniform(jax.random.fold_in(jax.random.fold_in(rng, 6), dim), (parts,), jnp.float32, least / len(split), largest / len(split))
        return jnp.repeat(jnp.exp(heights), shape[dim] // parts).reshape((-1,) + (1,) * (len(shape) - dim - 1))

    loudness = one(*split[0])
    for cut in split[1:]:
        loudness = loudness * one(*cut)
    return loudness


def noise(rng, dims, deviation, limit, split=(), kind=jnp.bfloat16):
    entries = jax.random.normal(rng, dims, jnp.float32) * deviation
    if len(split) > 0:
        entries = level_of(rng, dims, split, -0.22, 0.18) * entries
    return jnp.clip(entries, min=-limit, max=limit).astype(kind)


def setup_inputs(seed: int = 0) -> dict:
    seeds = jax.random.split(jax.random.key(seed), 13)
    return {
        "signal": draw_signal(jax.random.fold_in(seeds[12], 71), 0),
        "cotangent": noise(seeds[1], (STATIONS, FRAMES, D), 1.0, 6.0, ((0, 16), (1, 16))),
        "window_query": draw_window_query(jax.random.fold_in(seeds[12], 71), 0),
        "window_key": draw_window_key(jax.random.fold_in(seeds[12], 71), 0),
        "window_value": noise(seeds[4], (D, D), D ** -0.5, 0.375),
        "window_out": noise(seeds[5], (D, D), D ** -0.5, 0.375),
        "station_query": draw_station_query(jax.random.fold_in(seeds[12], 71), 0),
        "station_key": draw_station_key(jax.random.fold_in(seeds[12], 71), 0),
        "station_value": noise(seeds[8], (D, D), D ** -0.5, 0.375),
        "station_out": noise(seeds[9], (D, D), D ** -0.5, 0.375),
        "neighbours": set_ends(jax.random.randint(seeds[10], (STATIONS, NBR), 0, STATIONS), jax.random.fold_in(seeds[10], 1), 0, STATIONS - 1).astype(jnp.int32),
        "neighbour_valid": set_ends((jax.random.randint(seeds[11], (STATIONS, NBR), 0, 4) < 3).astype(jnp.int32), jax.random.fold_in(seeds[11], 1), 0, 1),
    }


def rounded_wide(values):
    narrow = lax.optimization_barrier(values.astype(jnp.bfloat16))
    return narrow.astype(jnp.float32)

def band_allowed(n_query, n_keys, half_width, first_frame, frames):
    rows = lax.broadcasted_iota(jnp.int32, (n_query, n_keys), 0)
    columns = lax.broadcasted_iota(jnp.int32, (n_query, n_keys), 1)
    offset = columns - rows
    frame_index = columns + first_frame
    return (offset >= 0) & (offset <= 2 * half_width) & (frame_index >= 0) & (frame_index < frames)

def neighbour_counts(neighbours, neighbour_valid, stations):
    targets = lax.broadcasted_iota(jnp.int32, (stations, neighbours.shape[1], stations), 2)
    listed = jnp.where((neighbours[:, :, None] == targets) & (neighbour_valid[:, :, None] == 1), 1.0, 0.0)
    diag_rows = lax.broadcasted_iota(jnp.int32, (stations, stations), 0)
    diag_cols = lax.broadcasted_iota(jnp.int32, (stations, stations), 1)
    itself = jnp.where(diag_rows == diag_cols, 1.0, 0.0)
    return (lax.optimization_barrier(jnp.sum(listed, axis=1)) + itself).astype(jnp.float32)

def window_probs(split_q, split_k, allowed, scale):
    scores = jnp.einsum('qhd,khd->hqk', split_q, split_k) * scale
    scores = jnp.where(allowed[None], scores, -1e+30)
    highest = lax.optimization_barrier(jnp.max(scores, axis=-1, keepdims=True))
    raised = jnp.exp(scores - highest)
    return raised / lax.optimization_barrier(jnp.sum(raised, axis=-1, keepdims=True))

def split_window(queries, kv_rows, heads):
    n_query, width_all = queries.shape
    head_size = width_all // heads
    split_q = queries.astype(jnp.float32).reshape(n_query, heads, head_size)
    split_k = kv_rows[:, :width_all].astype(jnp.float32).reshape(-1, heads, head_size)
    split_v = kv_rows[:, width_all:].astype(jnp.float32).reshape(-1, heads, head_size)
    return (split_q, split_k, split_v, 1.0 / math.sqrt(head_size))

def window_forward(queries, kv_rows, allowed, heads):
    n_query, width_all = queries.shape
    split_q, split_k, split_v, scale = split_window(queries, kv_rows, heads)
    weights = rounded_wide(window_probs(split_q, split_k, allowed, scale))
    mixed = jnp.einsum('hqk,khd->qhd', weights, split_v)
    return mixed.reshape(n_query, width_all).astype(jnp.bfloat16)

def window_backward(queries, kv_rows, allowed, grad_mix, heads):
    n_query, width_all = queries.shape
    split_q, split_k, split_v, scale = split_window(queries, kv_rows, heads)
    probs = window_probs(split_q, split_k, allowed, scale)
    weights = rounded_wide(probs)
    split_g = grad_mix.astype(jnp.float32).reshape(n_query, heads, -1)
    d_probs = jnp.einsum('qhd,khd->hqk', split_g, split_v)
    d_values = jnp.einsum('hqk,qhd->khd', weights, split_g)
    d_scores = probs * (d_probs - lax.optimization_barrier(jnp.sum(probs * d_probs, axis=-1, keepdims=True)))
    d_scores_b = rounded_wide(d_scores)
    d_queries = jnp.einsum('hqk,khd->qhd', d_scores_b, split_k) * scale
    d_keys = jnp.einsum('hqk,qhd->khd', d_scores_b, split_q) * scale
    n_keys = kv_rows.shape[0]
    d_kv = jnp.concatenate([d_keys.reshape(n_keys, width_all), d_values.reshape(n_keys, width_all)], axis=1)
    return (d_queries.reshape(n_query, width_all), d_kv)

def station_block(rows, grads, counts, station_query, station_key, station_value, station_out, heads):
    n_sta, n_frm, width_all = rows.shape
    head_size = width_all // heads
    scale = 1.0 / math.sqrt(head_size)
    qkv_weight = jnp.concatenate([station_query, station_key, station_value], axis=1)
    qkv = rounded_wide(jnp.dot(rows, qkv_weight, preferred_element_type=jnp.float32))
    split_q = qkv[..., :width_all].reshape(n_sta, n_frm, heads, head_size)
    split_k = qkv[..., width_all:2 * width_all].reshape(n_sta, n_frm, heads, head_size)
    split_v = qkv[..., 2 * width_all:].reshape(n_sta, n_frm, heads, head_size)
    scores = jnp.einsum('sfhd,tfhd->fhst', split_q, split_k) * scale
    scores = jnp.where(counts[None, None] > 0.0, scores, -1e+30)
    highest = lax.optimization_barrier(jnp.max(scores, axis=-1, keepdims=True))
    raised = counts[None, None] * jnp.exp(scores - highest)
    probs = raised / lax.optimization_barrier(jnp.sum(raised, axis=-1, keepdims=True))
    weights = rounded_wide(probs)
    mixed = jnp.einsum('fhst,tfhd->sfhd', weights, split_v).reshape(n_sta, n_frm, width_all)
    mix_narrow = lax.optimization_barrier(mixed.astype(jnp.bfloat16))
    output = (rows.astype(jnp.float32) + jnp.dot(mix_narrow, station_out, preferred_element_type=jnp.float32)).astype(jnp.bfloat16)
    grad_out = jnp.einsum('sfd,sfe->de', mix_narrow.astype(jnp.float32), grads.astype(jnp.float32))
    grad_mix = rounded_wide(jnp.dot(grads, station_out.T, preferred_element_type=jnp.float32))
    split_g = grad_mix.reshape(n_sta, n_frm, heads, head_size)
    d_probs = jnp.einsum('sfhd,tfhd->fhst', split_g, split_v)
    d_values = jnp.einsum('fhst,sfhd->tfhd', weights, split_g)
    d_scores = probs * (d_probs - lax.optimization_barrier(jnp.sum(probs * d_probs, axis=-1, keepdims=True)))
    d_scores_b = rounded_wide(d_scores)
    d_queries = jnp.einsum('fhst,tfhd->sfhd', d_scores_b, split_k) * scale
    d_keys = jnp.einsum('fhst,sfhd->tfhd', d_scores_b, split_q) * scale
    d_qkv = jnp.concatenate([d_queries.reshape(n_sta, n_frm, width_all), d_keys.reshape(n_sta, n_frm, width_all), d_values.reshape(n_sta, n_frm, width_all)], axis=2)
    d_qkv_b = lax.optimization_barrier(d_qkv.astype(jnp.bfloat16))
    grad_qkv = jnp.einsum('sfd,sfe->de', rows.astype(jnp.float32), d_qkv_b.astype(jnp.float32))
    grad_rows = (grads.astype(jnp.float32) + jnp.dot(d_qkv_b, qkv_weight.T, preferred_element_type=jnp.float32)).astype(jnp.bfloat16)
    return (output, grad_rows, grad_qkv, grad_out)

def reference(signal, cotangent, window_query, window_key, window_value, window_out, station_query, station_key, station_value, station_out, neighbours, neighbour_valid):
    kv_weight = jnp.concatenate([window_key, window_value], axis=1)
    n_blocks = FRAMES // FR_DEV
    key_span = FR_DEV + 2 * HALF
    block_ids = jnp.arange(n_blocks, dtype=jnp.int32)

    def station_window(rows):
        queries = jnp.dot(rows, window_query, preferred_element_type=jnp.float32).astype(jnp.bfloat16)
        kv_all = jnp.dot(rows, kv_weight, preferred_element_type=jnp.float32).astype(jnp.bfloat16)
        padded = jnp.pad(kv_all, ((HALF, HALF), (0, 0)))

        def one_block(block_index):
            first_row = block_index * FR_DEV
            q_block = lax.dynamic_slice_in_dim(queries, first_row, FR_DEV, 0)
            kv_block = lax.dynamic_slice_in_dim(padded, first_row, key_span, 0)
            allowed = band_allowed(FR_DEV, key_span, HALF, first_row - HALF, FRAMES)
            return window_forward(q_block, kv_block, allowed, HEADS)
        window_mix = lax.map(one_block, block_ids).reshape(FRAMES, D)
        return (queries, padded, window_mix)

    def first_phase(rows):
        queries, padded, window_mix = station_window(rows)
        return (rows.astype(jnp.float32) + jnp.dot(window_mix, window_out, preferred_element_type=jnp.float32)).astype(jnp.bfloat16)
    after_window = lax.map(first_phase, signal)
    counts = neighbour_counts(neighbours, neighbour_valid, STATIONS)
    n_groups = FRAMES // FR_STN

    def spatial_group(carry, group_index):
        first_row = group_index * FR_STN
        rows = lax.dynamic_slice_in_dim(after_window, first_row, FR_STN, 1)
        grads = lax.dynamic_slice_in_dim(cotangent, first_row, FR_STN, 1)
        output, grad_rows, grad_qkv, grad_out = station_block(rows, grads, counts, station_query, station_key, station_value, station_out, HEADS)
        return ((carry[0] + grad_qkv, carry[1] + grad_out), (output, grad_rows))
    start_sums = (jnp.zeros((D, 3 * D), jnp.float32), jnp.zeros((D, D), jnp.float32))
    station_sums, stacked = lax.scan(spatial_group, start_sums, jnp.arange(n_groups, dtype=jnp.int32))
    block_output = jnp.moveaxis(stacked[0], 0, 1).reshape(STATIONS, FRAMES, D)
    grad_after = jnp.moveaxis(stacked[1], 0, 1).reshape(STATIONS, FRAMES, D)

    def third_phase(operands):
        rows = operands[0]
        grad_rows = operands[1]
        queries, padded, window_mix = station_window(rows)
        grad_mix = jnp.dot(grad_rows, window_out.T, preferred_element_type=jnp.float32).astype(jnp.bfloat16)
        grad_out = jnp.dot(window_mix.T, grad_rows, preferred_element_type=jnp.float32)

        def one_block(carry, block_index):
            first_row = block_index * FR_DEV
            q_block = lax.dynamic_slice_in_dim(queries, first_row, FR_DEV, 0)
            kv_block = lax.dynamic_slice_in_dim(padded, first_row, key_span, 0)
            g_block = lax.dynamic_slice_in_dim(grad_mix, first_row, FR_DEV, 0)
            allowed = band_allowed(FR_DEV, key_span, HALF, first_row - HALF, FRAMES)
            d_query, d_kv = window_backward(q_block, kv_block, allowed, g_block, HEADS)
            current = lax.dynamic_slice_in_dim(carry, first_row, key_span, 0)
            return (lax.dynamic_update_slice_in_dim(carry, current + d_kv, first_row, 0), d_query)
        carry, d_queries = lax.scan(one_block, jnp.zeros((FRAMES + 2 * HALF, 2 * D), jnp.float32), block_ids)
        d_query = d_queries.reshape(FRAMES, D).astype(jnp.bfloat16)
        d_kv = carry[HALF:HALF + FRAMES].astype(jnp.bfloat16)
        grad_signal = grad_rows.astype(jnp.float32) + jnp.dot(d_query, window_query.T, preferred_element_type=jnp.float32) + jnp.dot(d_kv, kv_weight.T, preferred_element_type=jnp.float32)
        return (grad_signal.astype(jnp.bfloat16), jnp.dot(rows.T, d_query, preferred_element_type=jnp.float32), jnp.dot(rows.T, d_kv, preferred_element_type=jnp.float32), grad_out)
    signal_grad, grad_q_all, grad_kv_all, grad_o_all = lax.map(third_phase, (signal, grad_after))
    factor = 1.0 / math.sqrt(STATIONS * FRAMES)
    grad_wq = lax.optimization_barrier(jnp.sum(grad_q_all, axis=0)) * factor
    grad_wkv = lax.optimization_barrier(jnp.sum(grad_kv_all, axis=0)) * factor
    grad_wo = lax.optimization_barrier(jnp.sum(grad_o_all, axis=0)) * factor
    grad_sqkv = station_sums[0] * factor
    grad_so = station_sums[1] * factor
    return (block_output, signal_grad, grad_wq, grad_wkv[:, :D], grad_wkv[:, D:], grad_wo, grad_sqkv[:, :D], grad_sqkv[:, D:2 * D], grad_sqkv[:, 2 * D:], grad_so)
```

```python
import functools
import math

import jax
import jax.numpy as jnp
from jax import lax
from jax.experimental import pallas as pl
from jax.experimental.pallas import tpu as pltpu
from jax.sharding import PartitionSpec as P

MESH = pl.DeviceIdType.MESH
LANES = 128

HEADS = 4
HALF = 128


def with_halo(cells, sides, width):
    for axis, dim in sides:
        count = lax.axis_size(axis)
        ends = count - 1
        head = lax.slice_in_dim(cells, 0, width, axis=dim)
        tail = lax.slice_in_dim(cells, cells.shape[dim] - width, cells.shape[dim], axis=dim)
        cells = jnp.concatenate(
            [
                lax.ppermute(tail, axis, [(i, (i + 1) % count) for i in range(ends)]),
                cells,
                lax.ppermute(head, axis, [((i + 1) % count, i) for i in range(ends)]),
            ],
            axis=dim,
        )
    return cells


def band_allowed(n_query, n_keys, half_width, first_frame, frames):
    rows = lax.broadcasted_iota(jnp.int32, (n_query, n_keys), 0)
    columns = lax.broadcasted_iota(jnp.int32, (n_query, n_keys), 1)
    offset = columns - rows
    frame_index = columns + first_frame
    return (offset >= 0) & (offset <= 2 * half_width) & (frame_index >= 0) & (frame_index < frames)


def neighbour_counts(neighbours, neighbour_valid, stations):
    targets = lax.broadcasted_iota(jnp.int32, (stations, neighbours.shape[1], stations), 2)
    listed = jnp.where(
        (neighbours[:, :, None] == targets) & (neighbour_valid[:, :, None] == 1), 1.0, 0.0
    )
    diag_rows = lax.broadcasted_iota(jnp.int32, (stations, stations), 0)
    diag_cols = lax.broadcasted_iota(jnp.int32, (stations, stations), 1)
    itself = jnp.where(diag_rows == diag_cols, 1.0, 0.0)
    return (jnp.sum(listed, axis=1) + itself).astype(jnp.float32)


def window_probs(split_q, split_k, allowed, scale):
    scores = (
        jnp.einsum("qhd,khd->hqk", split_q, split_k, preferred_element_type=jnp.float32) * scale
    )
    scores = jnp.where(allowed[None], scores, -1e30)
    highest = jnp.max(scores, axis=-1, keepdims=True)
    raised = jnp.exp(scores - highest)
    return raised / jnp.sum(raised, axis=-1, keepdims=True)


def split_window(queries, kv_rows, heads):
    n_query, width_all = queries.shape
    head_size = width_all // heads
    split_q = queries.reshape(n_query, heads, head_size)
    split_k = kv_rows[:, :width_all].reshape(-1, heads, head_size)
    split_v = kv_rows[:, width_all:].reshape(-1, heads, head_size)
    return (split_q, split_k, split_v, 1.0 / math.sqrt(head_size))


def window_forward(queries, kv_rows, allowed, heads):
    n_query, width_all = queries.shape
    split_q, split_k, split_v, scale = split_window(queries, kv_rows, heads)
    weights = window_probs(split_q, split_k, allowed, scale).astype(jnp.bfloat16)
    mixed = jnp.einsum("hqk,khd->qhd", weights, split_v, preferred_element_type=jnp.float32)
    return mixed.reshape(n_query, width_all).astype(jnp.bfloat16)


def window_backward(queries, kv_rows, allowed, grad_mix, heads):
    n_query, width_all = queries.shape
    split_q, split_k, split_v, scale = split_window(queries, kv_rows, heads)
    scores = (
        jnp.einsum("qhd,khd->hqk", split_q, split_k, preferred_element_type=jnp.float32) * scale
    )
    scores = jnp.where(allowed[None], scores, -1e30)
    highest = jnp.max(scores, axis=-1, keepdims=True)
    raised = jnp.exp(scores - highest)
    totals = jnp.sum(raised, axis=-1, keepdims=True)
    probs = raised / totals
    weights = probs.astype(jnp.bfloat16)
    split_g = grad_mix.reshape(n_query, heads, -1)
    d_probs = jnp.einsum("qhd,khd->hqk", split_g, split_v, preferred_element_type=jnp.float32)
    d_values = jnp.einsum("hqk,qhd->khd", weights, split_g, preferred_element_type=jnp.float32)
    deltas = jnp.sum(probs * d_probs, axis=-1, keepdims=True)
    d_scores = probs * (d_probs - deltas)
    d_scores_b = d_scores.astype(jnp.bfloat16)
    d_queries = (
        jnp.einsum("hqk,khd->qhd", d_scores_b, split_k, preferred_element_type=jnp.float32) * scale
    )
    d_keys = (
        jnp.einsum("hqk,qhd->khd", d_scores_b, split_q, preferred_element_type=jnp.float32) * scale
    )
    n_keys = kv_rows.shape[0]
    d_kv = jnp.concatenate(
        [d_keys.reshape(n_keys, width_all), d_values.reshape(n_keys, width_all)], axis=1
    )
    normalizer = (highest + jnp.log(totals))[:, :, 0]
    row_stats = jnp.concatenate([normalizer.T, deltas[:, :, 0].T], axis=1)
    return (d_queries.reshape(n_query, width_all), d_kv, row_stats)


def station_block(
    rows, grads, counts, station_query, station_key, station_value, station_out, heads
):
    n_sta, n_frm, width_all = rows.shape
    head_size = width_all // heads
    scale = 1.0 / math.sqrt(head_size)
    qkv_weight = jnp.concatenate([station_query, station_key, station_value], axis=1)
    qkv = jnp.dot(rows, qkv_weight, preferred_element_type=jnp.float32).astype(jnp.bfloat16)
    split_q = qkv[..., :width_all].reshape(n_sta, n_frm, heads, head_size)
    split_k = qkv[..., width_all : 2 * width_all].reshape(n_sta, n_frm, heads, head_size)
    split_v = qkv[..., 2 * width_all :].reshape(n_sta, n_frm, heads, head_size)
    scores = (
        jnp.einsum("sfhd,tfhd->fhst", split_q, split_k, preferred_element_type=jnp.float32) * scale
    )
    scores = jnp.where(counts[None, None] > 0.0, scores, -1e30)
    highest = jnp.max(scores, axis=-1, keepdims=True)
    raised = counts[None, None] * jnp.exp(scores - highest)
    probs = raised / jnp.sum(raised, axis=-1, keepdims=True)
    weights = probs.astype(jnp.bfloat16)
    mixed = jnp.einsum("fhst,tfhd->sfhd", weights, split_v, preferred_element_type=jnp.float32)
    mix_narrow = mixed.reshape(n_sta, n_frm, width_all).astype(jnp.bfloat16)
    output = (
        rows.astype(jnp.float32)
        + jnp.dot(mix_narrow, station_out, preferred_element_type=jnp.float32)
    ).astype(jnp.bfloat16)
    grad_out = jnp.einsum("sfd,sfe->de", mix_narrow, grads, preferred_element_type=jnp.float32)
    grad_mix = jnp.dot(grads, station_out.T, preferred_element_type=jnp.float32).astype(
        jnp.bfloat16
    )
    split_g = grad_mix.reshape(n_sta, n_frm, heads, head_size)
    d_probs = jnp.einsum("sfhd,tfhd->fhst", split_g, split_v, preferred_element_type=jnp.float32)
    d_values = jnp.einsum("fhst,sfhd->tfhd", weights, split_g, preferred_element_type=jnp.float32)
    d_scores = probs * (d_probs - jnp.sum(probs * d_probs, axis=-1, keepdims=True))
    d_scores_b = d_scores.astype(jnp.bfloat16)
    d_queries = (
        jnp.einsum("fhst,tfhd->sfhd", d_scores_b, split_k, preferred_element_type=jnp.float32)
        * scale
    )
    d_keys = (
        jnp.einsum("fhst,sfhd->tfhd", d_scores_b, split_q, preferred_element_type=jnp.float32)
        * scale
    )
    d_qkv = jnp.concatenate(
        [
            d_queries.reshape(n_sta, n_frm, width_all),
            d_keys.reshape(n_sta, n_frm, width_all),
            d_values.reshape(n_sta, n_frm, width_all),
        ],
        axis=2,
    ).astype(jnp.bfloat16)
    grad_qkv = jnp.einsum("sfd,sfe->de", rows, d_qkv, preferred_element_type=jnp.float32)
    grad_rows = (
        grads.astype(jnp.float32) + jnp.dot(d_qkv, qkv_weight.T, preferred_element_type=jnp.float32)
    ).astype(jnp.bfloat16)
    return (output, grad_rows, grad_qkv, grad_out)


def place():
    stn = lax.axis_index("stn")
    tm = lax.axis_index("tm")
    core = stn % 2
    x = (stn // 2 % 2) * 2 + tm % 2
    return (stn // 4, x, tm // 2, core)


def device_at(y, x, z, core):
    return ((y * 2 + x // 2) * 2 + core, z * 2 + x % 2)


def sum_kernel(
    wq, wkv, wo, sqkv, so,
    o_wq, o_wk, o_wv, o_wo, o_sq, o_sk, o_sv, o_so,
    pack, final, from_core, half, from_plane, part, from_line,
    core_sem, plane_send, plane_recv, line_send, line_recv,
    back_core_sem, back_plane_send, back_plane_recv, back_line_send, back_line_recv,
    factor=1.0,
):
    y, x, z, core = place()
    other = device_at(y, x, z, 1 - core)
    plane_steps = [(dy, dx) for dy in range(4) for dx in range(4) if dy + dx > 0]
    plane_ids = [device_at((y + dy) % 4, (x + dx) % 4, z, core) for dy, dx in plane_steps]
    line_ids = [device_at(y, x, (z + dz) % 8, core) for dz in range(1, 8)]
    barrier = pltpu.get_barrier_semaphore()
    for peer in [other] + plane_ids + line_ids:
        pl.semaphore_signal(barrier, inc=1, device_id=peer, device_id_type=MESH)

    def send(src, dst, send_sem, recv_sem, peer):
        copy = pltpu.make_async_remote_copy(
            src_ref=src, dst_ref=dst, send_sem=send_sem, recv_sem=recv_sem,
            device_id=peer, device_id_type=MESH,
        )
        copy.start()
        return copy

    slabs = [(wq, 0), (wkv, 0), (wkv, 256), (wo, 0), (sqkv, 0), (sqkv, 256), (sqkv, 512), (so, 0)]
    for i, (ref, first) in enumerate(slabs):
        for j in range(2):
            pack[pl.ds((2 * i + j) * 256, 256), :] = ref[
                :, first + j * LANES : first + (j + 1) * LANES
            ].astype(jnp.bfloat16)
    pl.semaphore_wait(barrier, 1 + len(plane_ids) + len(line_ids))

    own_half = pl.multiple_of(core * 2048, 2048)
    other_half = pl.multiple_of((1 - core) * 2048, 2048)
    copy = send(
        pack.at[pl.ds(other_half, 2048)], from_core, core_sem.at[0], core_sem.at[1], other
    )
    copy.wait()
    half[...] = (
        pack[pl.ds(own_half, 2048), :].astype(jnp.float32) + from_core[...].astype(jnp.float32)
    ).astype(jnp.bfloat16)

    copies = []
    for k, (dy, dx) in enumerate(plane_steps):
        to = ((y + dy) % 4) * 4 + (x + dx) % 4
        copies.append(
            send(
                half.at[pl.ds(pl.multiple_of(to * 128, 128), 128)],
                from_plane.at[k],
                plane_send.at[k],
                plane_recv.at[k],
                plane_ids[k],
            )
        )
    mine = pl.multiple_of((y * 4 + x) * 128, 128)
    total = half[pl.ds(mine, 128), :].astype(jnp.float32)
    for k, copy in enumerate(copies):
        copy.wait_recv()
        total = total + from_plane[k].astype(jnp.float32)
    part[...] = total.astype(jnp.bfloat16)
    lines = []
    for k in range(7):
        to = (z + k + 1) % 8
        lines.append(
            send(
                part.at[pl.ds(pl.multiple_of(to * 16, 16), 16)],
                from_line.at[k],
                line_send.at[k],
                line_recv.at[k],
                line_ids[k],
            )
        )
    small = part[pl.ds(pl.multiple_of(z * 16, 16), 16), :].astype(jnp.float32)
    for k, copy in enumerate(lines):
        copy.wait_recv()
        small = small + from_line[k].astype(jnp.float32)
    base = pl.multiple_of(own_half + mine, 128)
    here = pl.ds(pl.multiple_of(base + z * 16, 16), 16)
    for copy in [*copies, *lines]:
        copy.wait_send()
    final[here, :] = small.astype(jnp.bfloat16)
    backs = [
        send(final.at[here], final.at[here], back_line_send.at[k], back_line_recv.at[k], line_ids[k])
        for k in range(7)
    ]
    for copy in backs:
        copy.wait()
    rows = pl.ds(base, 128)
    backs = [
        send(
            final.at[rows], final.at[rows], back_plane_send.at[k], back_plane_recv.at[k], plane_ids[k]
        )
        for k in range(15)
    ]
    for copy in backs:
        copy.wait()
    rows = pl.ds(own_half, 2048)
    send(final.at[rows], final.at[rows], back_core_sem.at[0], back_core_sem.at[1], other).wait()
    for i, ref in enumerate((o_wq, o_wk, o_wv, o_wo, o_sq, o_sk, o_sv, o_so)):
        for j in range(2):
            ref[:, j * LANES : (j + 1) * LANES] = (
                final[pl.ds((2 * i + j) * 256, 256), :].astype(jnp.float32) * factor
            )


def sum_gradients(wq, wkv, wo, sqkv, so, factor):
    dma = pltpu.SemaphoreType.DMA
    vmem = pl.BlockSpec(memory_space=pltpu.VMEM)
    return pl.pallas_call(
        functools.partial(sum_kernel, factor=factor),
        out_shape=[jax.ShapeDtypeStruct((256, 256), jnp.float32)] * 8,
        in_specs=[vmem] * 5,
        out_specs=[vmem] * 8,
        scratch_shapes=[
            pltpu.VMEM((4096, LANES), jnp.bfloat16),
            pltpu.VMEM((4096, LANES), jnp.bfloat16),
            pltpu.VMEM((2048, LANES), jnp.bfloat16),
            pltpu.VMEM((2048, LANES), jnp.bfloat16),
            pltpu.VMEM((15, 128, LANES), jnp.bfloat16),
            pltpu.VMEM((128, LANES), jnp.bfloat16),
            pltpu.VMEM((7, 16, LANES), jnp.bfloat16),
            dma((2,)), dma((15,)), dma((15,)), dma((7,)), dma((7,)),
            dma((2,)), dma((15,)), dma((15,)), dma((7,)), dma((7,)),
        ],
        compiler_params=pltpu.CompilerParams(collective_id=0, has_side_effects=True),
        name="sum_gradients",
    )(wq, wkv, wo, sqkv, so)


def body(
    signal,
    cotangent,
    window_query,
    window_key,
    window_value,
    window_out,
    station_query,
    station_key,
    station_value,
    station_out,
    neighbours,
    neighbour_valid,
):
    stn_local, frames_local, width_all = signal.shape
    half_width = HALF
    frames = frames_local * lax.axis_size("tm")
    stations = stn_local * lax.axis_size("stn")
    first_frame = lax.axis_index("tm") * frames_local - half_width
    kv_weight = jnp.concatenate([window_key, window_value], axis=1)
    queries = jnp.dot(signal, window_query, preferred_element_type=jnp.float32).astype(jnp.bfloat16)
    kv_local = jnp.dot(signal, kv_weight, preferred_element_type=jnp.float32).astype(jnp.bfloat16)
    kv_wide = with_halo(kv_local, (("tm", 1),), half_width)
    allowed = band_allowed(
        frames_local, frames_local + 2 * half_width, half_width, first_frame, frames
    )

    def forward_station(operands):
        return window_forward(operands[0], operands[1], allowed, HEADS)

    window_mix = lax.map(forward_station, (queries, kv_wide))
    after_window = (
        signal.astype(jnp.float32)
        + jnp.dot(window_mix, window_out, preferred_element_type=jnp.float32)
    ).astype(jnp.bfloat16)
    frame_rows = lax.all_to_all(after_window, "stn", split_axis=1, concat_axis=0, tiled=True)
    frame_grads = lax.all_to_all(cotangent, "stn", split_axis=1, concat_axis=0, tiled=True)
    counts = neighbour_counts(neighbours, neighbour_valid, stations)
    station_output, station_back, grad_sqkv, grad_so = station_block(
        frame_rows,
        frame_grads,
        counts,
        station_query,
        station_key,
        station_value,
        station_out,
        HEADS,
    )
    block_output = lax.all_to_all(station_output, "stn", split_axis=0, concat_axis=1, tiled=True)
    grad_after = lax.all_to_all(station_back, "stn", split_axis=0, concat_axis=1, tiled=True)
    grad_mix = jnp.dot(grad_after, window_out.T, preferred_element_type=jnp.float32).astype(
        jnp.bfloat16
    )
    grad_wo = jnp.einsum("sfd,sfe->de", window_mix, grad_after, preferred_element_type=jnp.float32)

    def backward_station(operands):
        return window_backward(operands[0], operands[1], allowed, operands[2], HEADS)

    d_query, d_kv_wide, row_stats = lax.map(backward_station, (queries, kv_wide, grad_mix))
    own_kv = d_kv_wide[:, half_width : half_width + frames_local]
    rims = jnp.concatenate(
        [d_kv_wide[:, :half_width], d_kv_wide[:, frames_local + half_width :]], axis=1
    )
    returned = with_halo(rims, (("tm", 1),), half_width)
    own_kv = own_kv.at[:, :half_width].add(returned[:, :half_width])
    own_kv = own_kv.at[:, frames_local - half_width :].add(returned[:, 3 * half_width :])
    d_query_b = d_query.astype(jnp.bfloat16)
    d_kv_b = own_kv.astype(jnp.bfloat16)
    grad_signal = (
        grad_after.astype(jnp.float32)
        + jnp.dot(d_query_b, window_query.T, preferred_element_type=jnp.float32)
        + jnp.dot(d_kv_b, kv_weight.T, preferred_element_type=jnp.float32)
    )
    signal_grad = grad_signal.astype(jnp.bfloat16)
    grad_wq = jnp.einsum("sfd,sfe->de", signal, d_query_b, preferred_element_type=jnp.float32)
    grad_wkv = jnp.einsum("sfd,sfe->de", signal, d_kv_b, preferred_element_type=jnp.float32)
    factor = 1.0 / math.sqrt(stations * frames)
    sums = sum_gradients(grad_wq, grad_wkv, grad_wo, grad_sqkv, grad_so, factor)
    return (block_output, signal_grad, *sums)


def solution(mesh):
    placed = (
        P("stn", "tm", None),
        P("stn", "tm", None),
        P(),
        P(),
        P(),
        P(),
        P(),
        P(),
        P(),
        P(),
        P(),
        P(),
    )
    return jax.shard_map(
        body,
        mesh=mesh,
        in_specs=placed,
        out_specs=(
            P("stn", "tm", None),
            P("stn", "tm", None),
            P(),
            P(),
            P(),
            P(),
            P(),
            P(),
            P(),
            P(),
        ),
        check_vma=False,
    )
```

```python
import functools
import math

import jax
import jax.numpy as jnp
from jax import lax
from jax.experimental import pallas as pl
from jax.experimental.pallas import tpu as pltpu
from jax.sharding import PartitionSpec as P

HEADS = 4
HALF = 128
LANES = 128
MESH = pl.DeviceIdType.MESH
F32 = jnp.float32
BF16 = jnp.bfloat16
STN = 16
TM = 16


def dot(a, b, kind="nn"):
    dims = {"nn": ((1,), (0,)), "nt": ((1,), (1,)), "tn": ((0,), (0,))}[kind]
    return lax.dot_general(a, b, (dims, ((), ())), preferred_element_type=F32)


def device_at(y, x, z, core):
    return ((y * 2 + x // 2) * 2 + core, z * 2 + x % 2)


def send(src, dst, send_sem, recv_sem, peer):
    copy = pltpu.make_async_remote_copy(
        src_ref=src,
        dst_ref=dst,
        send_sem=send_sem,
        recv_sem=recv_sem,
        device_id=peer,
        device_id_type=MESH,
    )
    copy.start()
    return copy


class Place:
    def __init__(self):
        self.stn = lax.axis_index("stn")
        self.tm = lax.axis_index("tm")
        self.core = self.stn % 2
        self.x = (self.stn // 2 % 2) * 2 + self.tm % 2
        self.y = self.stn // 4
        self.z = self.tm // 2
        y, x, z, core = self.y, self.x, self.z, self.core
        self.other = device_at(y, x, z, 1 - core)
        self.plane_steps = [(dy, dx) for dy in range(4) for dx in range(4) if dy + dx > 0]
        self.plane_ids = [
            device_at((y + dy) % 4, (x + dx) % 4, z, core) for dy, dx in self.plane_steps
        ]
        self.line_ids = [device_at(y, x, (z + dz) % 8, core) for dz in range(1, 8)]
        self.stn_ids = [((self.stn + r) % STN, self.tm) for r in range(1, STN)]
        self.left = (self.stn, (self.tm + TM - 1) % TM)
        self.right = (self.stn, (self.tm + 1) % TM)
        beside = (self.tm + TM - 1 + 2 * (self.stn // 8)) % TM
        self.rim_ids = [((self.stn + r) % STN, beside) for r in range(STN)]
        self.rim_sources = []
        for r in range(STN):
            source = (self.stn + STN - r) % STN
            self.rim_sources.append((source, (self.tm + TM + 1 - 2 * (source // 8)) % TM))


class Sum:
    def __init__(self, at, refs):
        self.at = at
        (
            self.pack, self.from_core, self.half, self.from_plane, self.line, self.fin,
            self.core_sem, self.plane_send, self.plane_recv, self.line_send, self.line_recv,
            self.back_send, self.back_recv, self.pass_send, self.pass_recv,
        ) = refs

    def put(self, index, value):
        for j in range(2):
            self.pack[pl.ds((2 * index + j) * 256, 256), :] = value[
                :, j * LANES : (j + 1) * LANES
            ].astype(BF16)

    def to_core(self):
        other_half = pl.multiple_of((1 - self.at.core) * 1024, 1024)
        self.first = send(
            self.pack.at[pl.ds(other_half, 1024)],
            self.from_core,
            self.core_sem.at[0],
            self.core_sem.at[1],
            self.at.other,
        )

    def to_plane(self):
        at = self.at
        self.first.wait()
        own_half = pl.multiple_of(at.core * 1024, 1024)
        self.half[...] = (
            self.pack[pl.ds(own_half, 1024), :].astype(F32) + self.from_core[...].astype(F32)
        ).astype(BF16)
        self.copies = []
        for k, (dy, dx) in enumerate(at.plane_steps):
            to = ((at.y + dy) % 4) * 4 + (at.x + dx) % 4
            self.copies.append(
                send(
                    self.half.at[pl.ds(pl.multiple_of(to * 64, 64), 64)],
                    self.from_plane.at[k],
                    self.plane_send.at[k],
                    self.plane_recv.at[k],
                    at.plane_ids[k],
                )
            )

    def to_line(self):
        at = self.at
        mine = pl.multiple_of((at.y * 4 + at.x) * 64, 64)
        total = self.half[pl.ds(mine, 64), :].astype(F32)
        for k, copy in enumerate(self.copies):
            copy.wait_recv()
            total = total + self.from_plane[k].astype(F32)
        self.line[at.z] = total.astype(BF16)
        self.lines = [
            send(
                self.line.at[at.z],
                self.line.at[at.z],
                self.line_send.at[k],
                self.line_recv.at[k],
                at.line_ids[k],
            )
            for k in range(7)
        ]

    def back(self):
        at = self.at
        for copy in self.lines:
            copy.wait_recv()
        total = self.line[0].astype(F32)
        for k in range(1, 8):
            total = total + self.line[k].astype(F32)
        mine = pl.multiple_of(at.core * 1024 + (at.y * 4 + at.x) * 64, 64)
        rows = self.fin.at[pl.ds(mine, 64)]
        self.fin[pl.ds(mine, 64), :] = total.astype(BF16)
        self.backs = [
            send(rows, rows, self.back_send.at[k], self.back_recv.at[k], at.plane_ids[k])
            for k in range(15)
        ]
        self.passes = [
            send(rows, rows, self.pass_send.at[15], self.pass_recv.at[15], at.other)
        ]

    def finish(self):
        at = self.at
        for k, (dy, dx) in enumerate(at.plane_steps):
            self.backs[k].wait_recv()
            came = ((at.y + 4 - dy) % 4) * 4 + (at.x + 4 - dx) % 4
            first = pl.multiple_of(at.core * 1024 + came * 64, 64)
            rows = self.fin.at[pl.ds(first, 64)]
            self.passes.append(
                send(rows, rows, self.pass_send.at[k], self.pass_recv.at[k], at.other)
            )
        for copy in self.passes:
            copy.wait()
        for copy in [*self.copies, *self.lines, *self.backs]:
            copy.wait_send()


def block_kernel(
    sig, cot, wq, wk, wv, wo, sq, sk, sv, so, nbr, val,
    bo_out, sg_out, fin_out,
    se, qe, ke, ve, me, lse, bias, pst, awb, mix_acc,
    rows_st, grads_st, cm, cb, qg, kg, vg, gg, acc_m, acc_q, acc_k, acc_v, flat,
    dq_b, dk_b, dv_b, mix_b, gr_st, bo_st, bo,
    gae, gme, delta, dq_acc, dk_acc, dv_acc,
    h_send, h_recv, a_send, a_recv, d_send, d_recv,
    *sum_refs,
):
    at = Place()
    barrier = pltpu.get_barrier_semaphore()
    known = [*at.stn_ids, at.left, at.right, *at.rim_sources, *at.plane_ids, *at.line_ids]
    for peer in known:
        pl.semaphore_signal(barrier, inc=1, device_id=peer, device_id_type=MESH)
    pl.semaphore_wait(barrier, len(known))
    station_sum = Sum(at, sum_refs[:15])
    window_sum = Sum(at, sum_refs[15:])

    def exchange(lane, source, target):
        return [
            send(
                source((at.stn + r) % STN),
                target(at.stn),
                a_send.at[lane, r - 1],
                a_recv.at[lane, r - 1],
                at.stn_ids[r - 1],
            )
            for r in range(1, STN)
        ]

    def sixteen(index):
        return pl.ds(pl.multiple_of(index * 16, 16), 16)

    halos = [
        send(sig.at[:, pl.ds(0, 128)], se.at[:, pl.ds(384, 128)], h_send.at[0], h_recv.at[0], at.left),
        send(sig.at[:, pl.ds(128, 128)], se.at[:, pl.ds(0, 128)], h_send.at[1], h_recv.at[1], at.right),
    ]
    to_frames = exchange(
        0, lambda d: cot.at[:, sixteen(d)], lambda m: grads_st.at[pl.ds(m * 2, 2)]
    )
    grads_st[pl.ds(at.stn * 2, 2)] = cot[:, sixteen(at.stn), :]

    scale = 0.125

    def project(s, first, rows):
        where = pl.ds(first, rows.shape[0])
        qe[s, where, :] = (dot(rows, wq[...]).astype(BF16) * scale).astype(BF16)
        ke[s, where, :] = dot(rows, wk[...]).astype(BF16)
        ve[s, where, :] = dot(rows, wv[...]).astype(BF16)

    for s in range(2):
        project(s, 128, sig[s])
    key = lax.broadcasted_iota(jnp.int32, (512, 256), 0)
    query = lax.broadcasted_iota(jnp.int32, (512, 256), 1)
    frame = key + (at.tm * 256 - HALF)
    seen = (key - query >= 0) & (key - query <= 2 * HALF) & (frame >= 0) & (frame < TM * 256)
    bias[...] = jnp.where(seen, 0.0, -1e30)
    target = lax.broadcasted_iota(jnp.int32, (32, 32), 1)
    counts = jnp.where(lax.broadcasted_iota(jnp.int32, (32, 32), 0) == target, 1.0, 0.0)
    for j in range(16):
        hit = (nbr[:, j : j + 1] == target) & (val[:, j : j + 1] == 1)
        counts = counts + jnp.where(hit, 1.0, 0.0)
    spread = jnp.where(
        lax.broadcasted_iota(jnp.int32, (256, 32), 0) // 8
        == lax.broadcasted_iota(jnp.int32, (256, 32), 1),
        1.0,
        0.0,
    ).astype(BF16)
    wide = dot(spread, dot(spread, counts.astype(BF16)).astype(BF16), "nt")
    same = (
        lax.broadcasted_iota(jnp.int32, (256, 256), 0) % 8
        == lax.broadcasted_iota(jnp.int32, (256, 256), 1) % 8
    )
    wide = jnp.where(same, wide, 0.0)
    cm[...] = wide
    cb[...] = jnp.where(wide > 0.0, 0.0, -1e30)

    lane_head = lax.broadcasted_iota(jnp.int32, (1, 256), 1) // 64

    def of_head(h):
        return jnp.where(lane_head == h, 1.0, 0.0).astype(BF16)

    for copy in halos:
        copy.wait_recv()
    for s in range(2):
        project(s, 0, se[s, 0:128, :])
        project(s, 384, se[s, 384:512, :])

    mix_acc[...] = jnp.zeros_like(mix_acc)

    def window_forward(i, carry):
        s, h = i // HEADS, i % HEADS
        mine = of_head(h)
        scores = dot(ke[s], qe[s, 128:384, :] * mine, "nt") + bias[...]
        highest = jnp.max(scores, axis=0, keepdims=True)
        raised = jnp.exp(scores - highest)
        total = jnp.sum(raised, axis=0, keepdims=True)
        probs = raised * (1.0 / total)
        pst[i] = probs
        lse[i, :, 128:384] = highest + jnp.log(total)
        mix_acc[s] += dot(probs.astype(BF16), ve[s] * mine, "tn")
        return carry

    lax.fori_loop(0, 2 * HEADS, window_forward, 0)
    for s in range(2):
        mixed = mix_acc[s].astype(BF16)
        me[s, 128:384, :] = mixed
        awb[s] = (sig[s].astype(F32) + dot(mixed, wo[...])).astype(BF16)
    to_rows = exchange(
        1, lambda d: awb.at[:, sixteen(d)], lambda m: rows_st.at[pl.ds(m * 2, 2)]
    )
    rows_st[pl.ds(at.stn * 2, 2)] = awb[:, sixteen(at.stn), :]
    rims = [
        send(me.at[:, pl.ds(128, 128)], me.at[:, pl.ds(384, 128)], h_send.at[2], h_recv.at[2], at.left),
        send(me.at[:, pl.ds(256, 128)], me.at[:, pl.ds(0, 128)], h_send.at[3], h_recv.at[3], at.right),
        send(lse.at[:, :, pl.ds(128, 128)], lse.at[:, :, pl.ds(384, 128)], h_send.at[4], h_recv.at[4], at.left),
        send(lse.at[:, :, pl.ds(256, 128)], lse.at[:, :, pl.ds(0, 128)], h_send.at[5], h_recv.at[5], at.right),
    ]

    def grouped(target_ref, value):
        parts = value.reshape(32, 2, 8, 256)
        for g in range(2):
            target_ref[g] = parts[:, g].reshape(256, 256).astype(BF16)

    for copy in to_frames:
        copy.wait_recv()
    grads = grads_st[...].reshape(512, 256)
    grouped(gg, dot(grads, so[...], "nt"))
    for ref in (acc_m, acc_q, acc_k, acc_v):
        ref[...] = jnp.zeros_like(ref)
    for copy in to_rows:
        copy.wait_recv()
    rows = rows_st[...].reshape(512, 256)
    grouped(qg, dot(rows, sq[...]).astype(BF16).astype(F32) * scale)
    grouped(kg, dot(rows, sk[...]))
    grouped(vg, dot(rows, sv[...]))

    def station(i, carry):
        g, h = i // HEADS, i % HEADS
        mine = of_head(h)
        q, k, v, gm = qg[g] * mine, kg[g] * mine, vg[g] * mine, gg[g] * mine
        scores = dot(k, q, "nt") + cb[...]
        highest = jnp.max(scores, axis=0, keepdims=True)
        raised = cm[...] * jnp.exp(scores - highest)
        probs = raised * (1.0 / jnp.sum(raised, axis=0, keepdims=True))
        weights = probs.astype(BF16)
        acc_m[g] += dot(weights, v, "tn")
        d_probs = dot(v, gm, "nt")
        moved = probs * d_probs
        d_scores = (moved - probs * jnp.sum(moved, axis=0, keepdims=True)).astype(BF16)
        acc_v[g] += dot(weights, gm)
        acc_q[g] += dot(d_scores, k, "tn")
        acc_k[g] += dot(d_scores, q)
        return carry

    lax.fori_loop(0, 2 * HEADS, station, 0)

    def ungroup(target_ref, acc, factor):
        for g in range(2):
            flat[:, g * 8 : (g + 1) * 8, :] = acc[g].reshape(32, 8, 256)
        value = flat[...].reshape(512, 256)
        if factor is not None:
            value = value * factor
        target_ref[...] = value.astype(BF16)

    ungroup(dq_b, acc_q, scale)
    ungroup(dk_b, acc_k, None)
    ungroup(dv_b, acc_v, None)
    ungroup(mix_b, acc_m, None)
    back_rows = (
        grads.astype(F32)
        + dot(dq_b[...], sq[...], "nt")
        + dot(dk_b[...], sk[...], "nt")
        + dot(dv_b[...], sv[...], "nt")
    )
    gr_st[...] = back_rows.astype(BF16).reshape(32, 16, 256)
    to_owner = exchange(
        2,
        lambda d: gr_st.at[pl.ds(d * 2, 2)],
        lambda m: gae.at[:, pl.ds(pl.multiple_of(128 + m * 16, 16), 16)],
    )
    rim_rows = pl.ds(pl.multiple_of((384 + at.stn * 16) % 512, 16), 16)
    to_rims = [
        send(
            gr_st.at[pl.ds((at.stn + r) % STN * 2, 2)],
            gae.at[:, rim_rows],
            d_send.at[r],
            d_recv.at[r],
            at.rim_ids[r],
        )
        for r in range(STN)
    ]
    gae[:, pl.ds(pl.multiple_of(128 + at.stn * 16, 16), 16), :] = gr_st[pl.ds(at.stn * 2, 2)]
    output = rows.astype(F32) + dot(mix_b[...], so[...])
    bo_st[...] = output.astype(BF16).reshape(32, 16, 256)
    to_output = exchange(
        3, lambda d: bo_st.at[pl.ds(d * 2, 2)], lambda m: bo.at[:, sixteen(m)]
    )
    bo[:, sixteen(at.stn), :] = bo_st[pl.ds(at.stn * 2, 2)]
    station_sum.put(0, dot(rows, dq_b[...], "tn"))
    station_sum.put(1, dot(rows, dk_b[...], "tn"))
    station_sum.put(2, dot(rows, dv_b[...], "tn"))
    station_sum.put(3, dot(mix_b[...], grads, "tn"))
    station_sum.to_core()

    for copy in rims:
        copy.wait_recv()
    for copy in [*to_owner, *to_rims]:
        copy.wait_recv()
    station_sum.to_plane()
    heads8 = jnp.where(
        lax.broadcasted_iota(jnp.int32, (8, 256), 1) // 64
        == lax.broadcasted_iota(jnp.int32, (8, 256), 0),
        1.0,
        0.0,
    ).astype(BF16)
    for s in range(2):
        gmix = dot(gae[s], wo[...], "nt").astype(BF16)
        gme[s] = gmix
        product = gmix.astype(F32) * me[s].astype(F32)
        high = product.astype(BF16)
        low = (product - high.astype(F32)).astype(BF16)
        sums = dot(heads8, high, "nt") + dot(heads8, low, "nt")
        for h in range(HEADS):
            delta[s * HEADS + h] = sums[h : h + 1, :]
    window_sum.put(
        3,
        dot(
            me[:, 128:384, :].reshape(512, 256), gae[:, 128:384, :].reshape(512, 256), "tn"
        ),
    )
    for ref in (dq_acc, dk_acc, dv_acc):
        ref[...] = jnp.zeros_like(ref)
    rim_key = lax.broadcasted_iota(jnp.int32, (128, 128), 0)
    rim_query = lax.broadcasted_iota(jnp.int32, (128, 128), 1)

    def window_backward(i, carry):
        s, h = i // HEADS, i % HEADS
        mine = of_head(h)
        q, k, g = qe[s] * mine, ke[s] * mine, gme[s] * mine
        v = ve[s]
        probs = pst[i]
        d_scores = (
            probs * (dot(v, g[128:384], "nt") - delta[i, :, 128:384])
        ).astype(BF16)
        weights = probs[128:384].astype(BF16)
        dq_acc[s] += dot(d_scores, k, "tn")
        d_key = dot(d_scores[128:384], q[128:384])
        d_value = dot(weights, g[128:384])

        def rim(keys, queries, allowed):
            scores = dot(k[keys : keys + 128], q[queries : queries + 128], "nt")
            scores = jnp.where(allowed, scores - lse[i, :, queries : queries + 128], -1e30)
            rim_probs = jnp.exp(scores)
            g_rim = g[queries : queries + 128]
            rim_scores = rim_probs * (
                dot(v[keys : keys + 128], g_rim, "nt") - delta[i, :, queries : queries + 128]
            )
            return (
                dot(rim_scores.astype(BF16), q[queries : queries + 128]),
                dot(rim_probs.astype(BF16), g_rim),
            )

        left_key, left_value = rim(128, 0, (rim_key <= rim_query) & (at.tm > 0))
        right_key, right_value = rim(256, 384, (rim_query <= rim_key) & (at.tm < TM - 1))
        dk_acc[s, 0:128, :] += d_key[0:128] + left_key
        dk_acc[s, 128:256, :] += d_key[128:256] + right_key
        dv_acc[s, 0:128, :] += d_value[0:128] + left_value
        dv_acc[s, 128:256, :] += d_value[128:256] + right_value
        return carry

    lax.fori_loop(0, 2 * HEADS, window_backward, 0)
    station_sum.to_line()
    signal = sig[...].reshape(512, 256)
    d_query = (dq_acc[...].reshape(512, 256) * scale).astype(BF16)
    d_key = dk_acc[...].reshape(512, 256).astype(BF16)
    d_value = dv_acc[...].reshape(512, 256).astype(BF16)
    window_sum.put(0, dot(signal, d_query, "tn"))
    window_sum.put(1, dot(signal, d_key, "tn"))
    window_sum.put(2, dot(signal, d_value, "tn"))
    window_sum.to_core()
    signal_grad = (
        gae[:, 128:384, :].reshape(512, 256).astype(F32)
        + dot(d_query, wq[...], "nt")
        + dot(d_key, wk[...], "nt")
        + dot(d_value, wv[...], "nt")
    )
    sg_out[...] = signal_grad.astype(BF16).reshape(2, 256, 256)
    window_sum.to_plane()
    station_sum.back()
    window_sum.to_line()
    window_sum.back()
    station_sum.finish()
    for copy in to_output:
        copy.wait_recv()
    bo_out[...] = bo[...]
    window_sum.finish()
    for copy in [*halos, *to_frames, *to_rows, *rims, *to_owner, *to_rims, *to_output]:
        copy.wait_send()
    fin_out[0:2048, :] = window_sum.fin[...]
    fin_out[2048:4096, :] = station_sum.fin[...]


def sum_scratch():
    dma = pltpu.SemaphoreType.DMA
    return [
        pltpu.VMEM((2048, LANES), BF16),
        pltpu.VMEM((1024, LANES), BF16),
        pltpu.VMEM((1024, LANES), BF16),
        pltpu.VMEM((15, 64, LANES), BF16),
        pltpu.VMEM((8, 64, LANES), BF16),
        pltpu.VMEM((2048, LANES), BF16),
        dma((2,)), dma((15,)), dma((15,)), dma((7,)), dma((7,)),
        dma((15,)), dma((15,)), dma((16,)), dma((16,)),
    ]


def finish_kernel(factor, bo, sg, fin, o_bo, o_sg, o_wq, o_wk, o_wv, o_wo, o_sq, o_sk, o_sv, o_so):
    o_bo[...] = bo[...]
    o_sg[...] = sg[...]
    for i, ref in enumerate((o_wq, o_wk, o_wv, o_wo, o_sq, o_sk, o_sv, o_so)):
        for j in range(2):
            ref[:, j * LANES : (j + 1) * LANES] = (
                fin[pl.ds((2 * i + j) * 256, 256), :].astype(F32) * factor
            )


def body(signal, cotangent, *rest):
    dma = pltpu.SemaphoreType.DMA
    vmem = pl.BlockSpec(memory_space=pltpu.VMEM)

    def b(*shape):
        return pltpu.VMEM(shape, BF16)

    def f(*shape):
        return pltpu.VMEM(shape, F32)

    scratch = [
        b(2, 512, 256), b(2, 512, 256), b(2, 512, 256), b(2, 512, 256), b(2, 512, 256),
        f(8, 1, 512), f(512, 256), f(8, 512, 256), b(2, 256, 256), f(2, 256, 256),
        b(32, 16, 256), b(32, 16, 256), f(256, 256), f(256, 256),
        b(2, 256, 256), b(2, 256, 256), b(2, 256, 256), b(2, 256, 256),
        f(2, 256, 256), f(2, 256, 256), f(2, 256, 256), f(2, 256, 256), f(32, 16, 256),
        b(512, 256), b(512, 256), b(512, 256), b(512, 256),
        b(32, 16, 256), b(32, 16, 256), b(2, 256, 256),
        b(2, 512, 256), b(2, 512, 256), f(8, 1, 512),
        f(2, 256, 256), f(2, 256, 256), f(2, 256, 256),
        dma((6,)), dma((6,)), dma((4, 15)), dma((4, 15)), dma((16,)), dma((16,)),
        *sum_scratch(), *sum_scratch(),
    ]
    block_output, signal_grad, fin = pl.pallas_call(
        block_kernel,
        out_shape=[
            jax.ShapeDtypeStruct((2, 256, 256), BF16),
            jax.ShapeDtypeStruct((2, 256, 256), BF16),
            jax.ShapeDtypeStruct((4096, LANES), BF16),
        ],
        in_specs=[vmem] * 12,
        out_specs=[vmem] * 3,
        scratch_shapes=scratch,
        compiler_params=pltpu.CompilerParams(
            collective_id=0, has_side_effects=True, vmem_limit_bytes=48 * 1024 * 1024
        ),
        name="block",
    )(signal, cotangent, *rest)
    factor = 1.0 / math.sqrt(STN * 2 * TM * 256)
    return pl.pallas_call(
        functools.partial(finish_kernel, factor),
        out_shape=[
            jax.ShapeDtypeStruct((2, 256, 256), BF16),
            jax.ShapeDtypeStruct((2, 256, 256), BF16),
        ]
        + [jax.ShapeDtypeStruct((256, 256), F32)] * 8,
        in_specs=[vmem] * 3,
        out_specs=[vmem] * 10,
        name="finish",
    )(block_output, signal_grad, fin)


def solution(mesh):
    return jax.shard_map(
        lambda *operands: tuple(body(*operands)),
        mesh=mesh,
        in_specs=(P("stn", "tm", None), P("stn", "tm", None), *([P()] * 10)),
        out_specs=(P("stn", "tm", None), P("stn", "tm", None), *([P()] * 8)),
        check_vma=False,
    )
```

```python
import functools
import math

import jax
import jax.numpy as jnp
from jax import lax
from jax.experimental import pallas as pl
from jax.experimental.pallas import tpu as pltpu
from jax.sharding import PartitionSpec as P

HEADS = 4
HALF = 128
LANES = 128
MESH = pl.DeviceIdType.MESH
F32 = jnp.float32
BF16 = jnp.bfloat16
STN = 16
TM = 16


def rem(a, n):
    return lax.rem(a, jnp.int32(n))


def div(a, n):
    return lax.div(a, jnp.int32(n))


def dot(a, b, kind="nn"):
    dims = {"nn": ((1,), (0,)), "nt": ((1,), (1,)), "tn": ((0,), (0,))}[kind]
    return lax.dot_general(a, b, (dims, ((), ())), preferred_element_type=F32)


def device_at(y, x, z, core):
    return ((y * 2 + div(x, 2)) * 2 + core, z * 2 + rem(x, 2))


def send(src, dst, send_sem, recv_sem, peer):
    copy = pltpu.make_async_remote_copy(
        src_ref=src,
        dst_ref=dst,
        send_sem=send_sem,
        recv_sem=recv_sem,
        device_id=peer,
        device_id_type=MESH,
    )
    copy.start()
    return copy


class Place:
    def __init__(self):
        self.stn = lax.axis_index("stn")
        self.tm = lax.axis_index("tm")
        self.core = rem(self.stn, 2)
        self.x = rem(div(self.stn, 2), 2) * 2 + rem(self.tm, 2)
        self.y = div(self.stn, 4)
        self.z = div(self.tm, 2)
        y, x, z, core = self.y, self.x, self.z, self.core
        self.other = device_at(y, x, z, 1 - core)
        self.plane_steps = [(dy, dx) for dy in range(4) for dx in range(4) if dy + dx > 0]
        ys = [rem(y + d, 4) for d in range(4)]
        xs = [rem(x + d, 4) for d in range(4)]
        zs = [rem(z + d, 8) for d in range(8)]
        self.plane_to = [ys[dy] * 4 + xs[dx] for dy, dx in self.plane_steps]
        self.plane_from = [ys[-dy % 4] * 4 + xs[-dx % 4] for dy, dx in self.plane_steps]
        self.plane_ids = [device_at(ys[dy], xs[dx], z, core) for dy, dx in self.plane_steps]
        self.line_ids = [device_at(y, x, zs[d], core) for d in range(1, 8)]
        self.stns = [rem(self.stn + r, STN) for r in range(STN)]
        self.stn_ids = [(self.stns[r], self.tm) for r in range(1, STN)]
        self.left = (self.stn, rem(self.tm + TM - 1, TM))
        self.right = (self.stn, rem(self.tm + 1, TM))
        beside = rem(self.tm + TM - 1 + 2 * div(self.stn, 8), TM)
        self.rim_ids = [(self.stns[r], beside) for r in range(STN)]
        self.rim_sources = []
        for r in range(STN):
            source = self.stns[-r % STN]
            self.rim_sources.append((source, rem(self.tm + TM + 1 - 2 * div(source, 8), TM)))


class Sum:
    def __init__(self, at, count, refs):
        self.at = at
        self.rows = count * 16
        self.half_rows = count * 256
        (
            self.pack, self.from_core, self.half, self.from_plane, self.line, self.fin,
            self.core_sem, self.plane_send, self.plane_recv, self.line_send, self.line_recv,
            self.back_send, self.back_recv, self.pass_send, self.pass_recv,
        ) = refs

    def put(self, index, value):
        for j in range(2):
            self.pack[pl.ds((2 * index + j) * 256, 256), :] = value[
                :, j * LANES : (j + 1) * LANES
            ].astype(BF16)

    def slot(self, index):
        return pl.ds(pl.multiple_of(index * self.rows, self.rows), self.rows)

    def final(self, index):
        first = self.at.core * self.half_rows + index * self.rows
        return pl.ds(pl.multiple_of(first, self.rows), self.rows)

    def to_core(self):
        other_half = pl.multiple_of((1 - self.at.core) * self.half_rows, self.half_rows)
        self.first = send(
            self.pack.at[pl.ds(other_half, self.half_rows)],
            self.from_core,
            self.core_sem.at[0],
            self.core_sem.at[1],
            self.at.other,
        )

    def to_plane(self):
        at = self.at
        self.first.wait()
        own_half = pl.multiple_of(at.core * self.half_rows, self.half_rows)
        self.half[...] = (
            self.pack[pl.ds(own_half, self.half_rows), :].astype(F32)
            + self.from_core[...].astype(F32)
        ).astype(BF16)
        self.copies = [
            send(
                self.half.at[self.slot(at.plane_to[k])],
                self.from_plane.at[k],
                self.plane_send.at[k],
                self.plane_recv.at[k],
                at.plane_ids[k],
            )
            for k in range(15)
        ]

    def to_line(self):
        at = self.at
        total = self.half[self.slot(at.y * 4 + at.x), :].astype(F32)
        for k, copy in enumerate(self.copies):
            copy.wait_recv()
            total = total + self.from_plane[k].astype(F32)
        self.line[at.z] = total.astype(BF16)
        self.lines = [
            send(
                self.line.at[at.z],
                self.line.at[at.z],
                self.line_send.at[k],
                self.line_recv.at[k],
                at.line_ids[k],
            )
            for k in range(7)
        ]

    def back(self):
        at = self.at
        for copy in self.lines:
            copy.wait_recv()
        total = self.line[0].astype(F32)
        for k in range(1, 8):
            total = total + self.line[k].astype(F32)
        mine = self.final(at.y * 4 + at.x)
        rows = self.fin.at[mine]
        self.fin[mine, :] = total.astype(BF16)
        self.backs = [
            send(rows, rows, self.back_send.at[k], self.back_recv.at[k], at.plane_ids[k])
            for k in range(15)
        ]
        self.passes = [
            send(rows, rows, self.pass_send.at[15], self.pass_recv.at[15], at.other)
        ]

    def pass_on(self):
        at = self.at
        for k in range(15):
            self.backs[k].wait_recv()
            rows = self.fin.at[self.final(at.plane_from[k])]
            self.passes.append(
                send(rows, rows, self.pass_send.at[k], self.pass_recv.at[k], at.other)
            )

    def finish(self):
        for copy in self.passes:
            copy.wait()
        for copy in [*self.copies, *self.lines, *self.backs]:
            copy.wait_send()


def iota(shape, dim):
    return lax.broadcasted_iota(jnp.int32, shape, dim)


def four(value):
    return jnp.concatenate([value] * HEADS, axis=1)


def stack(rows):
    head = iota((1, 256), 1) // 64
    return jnp.concatenate(
        [rows * jnp.where(head == h, 1.0, 0.0).astype(BF16) for h in range(HEADS)], axis=0
    )


def by_rows(tile):
    return jnp.concatenate([tile[:, h * 128 : (h + 1) * 128] for h in range(HEADS)], axis=0)


def block_kernel(
    sig_in, cot, wq_in, wk_in, wv_in, wo_in, sq_in, sk_in, sv_in, so_in, nbr_in, val_in,
    bo_out, sg_out, fin_out,
    sig, weights, nbr, val,
    se, qe, ke, ve, me, lse, bias_own, bias_halo, bias_rim, own_top, own_sum,
    probs_own, probs_halo, probs_rim, awb,
    rows_st, grads_st, cm, cb, perm, perm_back, qg, kg, vg, gg,
    dq_b, dk_b, dv_b, mix_b, gr_st, bo_st, bo,
    gae, gme, delta, dq_w,
    in_sem, h_send, h_recv, a_send, a_recv, d_send, d_recv,
    *sum_refs,
):
    wq, wk, wv, wo, sq, sk, sv, so = (weights.at[i] for i in range(8))
    fetches = [pltpu.make_async_copy(sig_in, sig, in_sem.at[0])]
    for i, ref in enumerate((wq_in, wk_in, wv_in, wo_in, sq_in, sk_in, sv_in, so_in)):
        fetches.append(pltpu.make_async_copy(ref, weights.at[i], in_sem.at[1 + i]))
    fetches.append(pltpu.make_async_copy(nbr_in, nbr, in_sem.at[9]))
    fetches.append(pltpu.make_async_copy(val_in, val, in_sem.at[10]))
    for copy in fetches:
        copy.start()
    at = Place()
    barrier = pltpu.get_barrier_semaphore()
    known = [at.left, at.right, *at.stn_ids, *at.rim_sources, *at.plane_ids, *at.line_ids]
    for peer in known:
        pl.semaphore_signal(barrier, inc=1, device_id=peer, device_id_type=MESH)

    def sixteen(index, base=0):
        return pl.ds(pl.multiple_of(base + index * 16, 16), 16)

    own_cot = pltpu.make_async_copy(
        cot.at[:, sixteen(at.stn)], grads_st.at[pl.ds(at.stn * 2, 2)], in_sem.at[11]
    )
    own_cot.start()
    pl.semaphore_wait(barrier, len(known))
    station_sum = Sum(at, 5, sum_refs[:15])
    window_sum = Sum(at, 3, sum_refs[15:])

    def exchange(lane, source, target):
        return [
            send(
                source(at.stns[r]),
                target(at.stn),
                a_send.at[lane, r - 1],
                a_recv.at[lane, r - 1],
                at.stn_ids[r - 1],
            )
            for r in range(1, STN)
        ]

    def beside(lane, first, last, to_right, to_left):
        return [
            send(first, to_left, h_send.at[lane], h_recv.at[lane], at.left),
            send(last, to_right, h_send.at[lane + 1], h_recv.at[lane + 1], at.right),
        ]

    halos = beside(
        0,
        sig_in.at[:, pl.ds(0, 128)],
        sig_in.at[:, pl.ds(128, 128)],
        se.at[:, pl.ds(0, 128)],
        se.at[:, pl.ds(384, 128)],
    )
    for copy in fetches:
        copy.wait()
    scale = 0.125

    def project(s, first, rows):
        where = pl.ds(first, rows.shape[0])
        qe[s, where, :] = (dot(rows, wq[...]).astype(BF16) * scale).astype(BF16)
        ke[s, where, :] = dot(rows, wk[...]).astype(BF16)
        ve[s, where, :] = dot(rows, wv[...]).astype(BF16)

    for s in range(2):
        project(s, 128, sig[s])
    low = -1e30
    key = iota((256, 128), 0)
    query = iota((256, 128), 1)
    for half in range(2):
        offset = key - query - 128 * half
        bias_own[half] = four(jnp.where((offset <= HALF) & (offset >= -HALF), 0.0, low))
    key = iota((128, 128), 0)
    query = iota((128, 128), 1)
    has_left = at.tm > 0
    has_right = at.tm < TM - 1
    bias_halo[0] = four(jnp.where((key >= query) & has_left, 0.0, low))
    bias_halo[1] = four(jnp.where((key <= query) & has_right, 0.0, low))
    bias_rim[0] = four(jnp.where((key <= query) & has_left, 0.0, low))
    bias_rim[1] = four(jnp.where((key >= query) & has_right, 0.0, low))

    def own_scores(unit, carry):
        s, half = unit // 2, unit % 2
        queries = stack(qe[s, pl.ds(pl.multiple_of(128 + half * 128, 128), 128), :])
        scores = dot(ke[s, 128:384, :], queries, "nt") + bias_own[half]
        top = jnp.max(scores, axis=0, keepdims=True)
        raised = jnp.exp(scores - top)
        probs_own[unit] = raised
        own_top[unit] = top
        own_sum[unit] = jnp.sum(raised, axis=0, keepdims=True)
        return carry

    lax.fori_loop(0, 4, own_scores, 0)
    to_frames = exchange(
        0, lambda d: cot.at[:, sixteen(d)], lambda m: grads_st.at[pl.ds(m * 2, 2)]
    )
    target = iota((32, 32), 0)
    counts = jnp.where(iota((32, 32), 1) == target, 1.0, 0.0)
    for j in range(16):
        hit = (nbr[j : j + 1, :] == target) & (val[j : j + 1, :] == 1)
        counts = counts + jnp.where(hit, 1.0, 0.0)
    spread = jnp.where(iota((128, 32), 0) // 4 == iota((128, 32), 1), 1.0, 0.0).astype(BF16)
    wide = dot(dot(spread, counts.astype(BF16)).astype(BF16), spread, "nt")
    wide = jnp.where(iota((128, 128), 0) % 4 == iota((128, 128), 1) % 4, wide, 0.0)
    cm[...] = four(wide)
    cb[...] = four(jnp.where(wide > 0.0, 0.0, low))

    def placed(row):
        return row % 128 // 4 * 16 + row // 128 * 4 + row % 4

    perm[...] = jnp.where(placed(iota((512, 1), 0)) == iota((512, 512), 1), 1.0, 0.0).astype(BF16)
    perm_back[...] = jnp.where(
        placed(iota((1, 512), 1)) == iota((512, 512), 0), 1.0, 0.0
    ).astype(BF16)

    for copy in halos:
        copy.wait_recv()
    to_rows = []
    for s in range(2):
        project(s, 0, se[s, 0:128, :])
        project(s, 384, se[s, 384:512, :])
        for half in range(2):
            unit = 2 * s + half
            halo = 384 * half
            queries = stack(qe[s, 128 + half * 128 : 256 + half * 128, :])
            scores = dot(ke[s, halo : halo + 128, :], queries, "nt") + bias_halo[half]
            top = jnp.maximum(own_top[unit], jnp.max(scores, axis=0, keepdims=True))
            raised = jnp.exp(scores - top)
            shift = jnp.exp(own_top[unit] - top)
            total = own_sum[unit] * shift + jnp.sum(raised, axis=0, keepdims=True)
            lse[1 + half, s] = top + jnp.log(total)
            inverse = 1.0 / total
            p_own = probs_own[unit] * (shift * inverse)
            p_halo = raised * inverse
            probs_own[unit] = p_own
            probs_halo[unit] = p_halo
            mixed = (
                dot(by_rows(p_own.astype(BF16)), stack(ve[s, 128:384, :]), "tn")
                + dot(by_rows(p_halo.astype(BF16)), stack(ve[s, halo : halo + 128, :]), "tn")
            ).astype(BF16)
            me[s, 128 + half * 128 : 256 + half * 128, :] = mixed
        awb[s] = (sig[s].astype(F32) + dot(me[s, 128:384, :], wo[...])).astype(BF16)
        to_rows += exchange(
            1 + s, lambda d: awb.at[s, sixteen(d)], lambda m: rows_st.at[m * 2 + s]
        )
    rows_st[pl.ds(at.stn * 2, 2)] = awb[:, sixteen(at.stn), :]

    own_cot.wait()
    for copy in to_frames:
        copy.wait_recv()
    grads = dot(perm[...], grads_st[...].reshape(512, 256)).astype(BF16)
    gg[...] = dot(grads, so[...], "nt").astype(BF16)
    for copy in to_rows:
        copy.wait_recv()
    rims = [
        *beside(
            2,
            me.at[:, pl.ds(128, 128)],
            me.at[:, pl.ds(256, 128)],
            me.at[:, pl.ds(0, 128)],
            me.at[:, pl.ds(384, 128)],
        ),
        *beside(4, lse.at[1], lse.at[2], lse.at[0], lse.at[3]),
    ]
    rows = dot(perm[...], rows_st[...].reshape(512, 256)).astype(BF16)
    qg[...] = (dot(rows, sq[...]).astype(BF16) * scale).astype(BF16)
    kg[...] = dot(rows, sk[...]).astype(BF16)
    vg[...] = dot(rows, sv[...]).astype(BF16)

    def station(g, carry):
        part = pl.ds(pl.multiple_of(g * 128, 128), 128)
        k, v = kg[part, :], vg[part, :]
        q4, g4 = stack(qg[part, :]), stack(gg[part, :])
        scores = dot(k, q4, "nt") + cb[...]
        raised = cm[...] * jnp.exp(scores - jnp.max(scores, axis=0, keepdims=True))
        probs = raised * (1.0 / jnp.sum(raised, axis=0, keepdims=True))
        narrow = probs.astype(BF16)
        mix_b[part, :] = dot(by_rows(narrow), stack(v), "tn").astype(BF16)
        moved = probs * dot(v, g4, "nt")
        d_scores = (moved - probs * jnp.sum(moved, axis=0, keepdims=True)).astype(BF16)
        dv_b[part, :] = dot(narrow, g4).astype(BF16)
        dq_b[part, :] = (dot(by_rows(d_scores), stack(k), "tn") * scale).astype(BF16)
        dk_b[part, :] = dot(d_scores, q4).astype(BF16)
        return carry

    lax.fori_loop(0, 4, station, 0)
    back_rows = (
        grads.astype(F32)
        + dot(dq_b[...], sq[...], "nt")
        + dot(dk_b[...], sk[...], "nt")
        + dot(dv_b[...], sv[...], "nt")
    ).astype(BF16)
    gr_st[...] = dot(perm_back[...], back_rows).astype(BF16).reshape(32, 16, 256)
    to_owner = exchange(
        3, lambda d: gr_st.at[pl.ds(d * 2, 2)], lambda m: gae.at[:, sixteen(m, 128)]
    )
    rim_rows = pl.ds(pl.multiple_of(rem(384 + at.stn * 16, 512), 16), 16)
    to_rims = [
        send(
            gr_st.at[pl.ds(at.stns[r] * 2, 2)],
            gae.at[:, rim_rows],
            d_send.at[r],
            d_recv.at[r],
            at.rim_ids[r],
        )
        for r in range(STN)
    ]
    gae[:, sixteen(at.stn, 128), :] = gr_st[pl.ds(at.stn * 2, 2)]
    output = (rows.astype(F32) + dot(mix_b[...], so[...])).astype(BF16)
    bo_st[...] = dot(perm_back[...], output).astype(BF16).reshape(32, 16, 256)
    bo[:, sixteen(at.stn), :] = bo_st[pl.ds(at.stn * 2, 2)]
    station_sum.put(0, dot(rows, dq_b[...], "tn"))
    station_sum.put(1, dot(rows, dk_b[...], "tn"))
    station_sum.put(2, dot(rows, dv_b[...], "tn"))
    station_sum.put(3, dot(mix_b[...], grads, "tn"))

    for copy in rims:
        copy.wait_recv()

    def rim_scores(unit, carry):
        s, side = unit // 2, unit % 2
        queries = stack(qe[s, pl.ds(pl.multiple_of(384 * side, 128), 128), :])
        keys = ke[s, pl.ds(pl.multiple_of(128 + side * 128, 128), 128), :]
        scores = dot(keys, queries, "nt") + bias_rim[side]
        probs_rim[unit] = jnp.exp(scores - lse[3 * side, s])
        return carry

    lax.fori_loop(0, 4, rim_scores, 0)
    for copy in [*to_owner, *to_rims]:
        copy.wait_recv()
    to_output = exchange(
        4, lambda d: bo_st.at[pl.ds(d * 2, 2)], lambda m: bo.at[:, sixteen(m)]
    )
    heads8 = jnp.where(iota((8, 256), 1) // 64 == iota((8, 256), 0), 1.0, 0.0).astype(BF16)
    for s in range(2):
        gmix = dot(gae[s], wo[...], "nt").astype(BF16)
        gme[s] = gmix
        product = gmix.astype(F32) * me[s].astype(F32)
        high = product.astype(BF16)
        rest = (product - high.astype(F32)).astype(BF16)
        sums = dot(heads8, high, "nt") + dot(heads8, rest, "nt")
        for slot in range(4):
            for h in range(HEADS):
                delta[slot, s, :, h * 128 : (h + 1) * 128] = sums[
                    h : h + 1, slot * 128 : (slot + 1) * 128
                ]
    own_grads = gae[:, 128:384, :].reshape(512, 256)
    station_sum.put(4, dot(me[:, 128:384, :].reshape(512, 256), own_grads, "tn"))
    station_sum.to_core()

    for s in range(2):
        d_key = jnp.zeros((256, 256), F32)
        d_value = jnp.zeros((256, 256), F32)
        for half in range(2):
            unit = 2 * s + half
            halo = 384 * half
            first = 128 + half * 128
            g4 = stack(gme[s, first : first + 128, :])
            q4 = stack(qe[s, first : first + 128, :])
            p_own, p_halo = probs_own[unit], probs_halo[unit]
            drop = delta[1 + half, s]
            ds_own = (p_own * (dot(ve[s, 128:384, :], g4, "nt") - drop)).astype(BF16)
            ds_halo = (p_halo * (dot(ve[s, halo : halo + 128, :], g4, "nt") - drop)).astype(BF16)
            dq_w[s, half * 128 : half * 128 + 128, :] = (
                (
                    dot(by_rows(ds_own), stack(ke[s, 128:384, :]), "tn")
                    + dot(by_rows(ds_halo), stack(ke[s, halo : halo + 128, :]), "tn")
                )
                * scale
            ).astype(BF16)
            d_key = d_key + dot(ds_own, q4)
            d_value = d_value + dot(p_own.astype(BF16), g4)
        rim_key, rim_value = [], []
        for side in range(2):
            rim = 384 * side
            g4 = stack(gme[s, rim : rim + 128, :])
            q4 = stack(qe[s, rim : rim + 128, :])
            p_rim = probs_rim[2 * s + side]
            values = ve[s, 128 + side * 128 : 256 + side * 128, :]
            ds_rim = (p_rim * (dot(values, g4, "nt") - delta[3 * side, s])).astype(BF16)
            rim_key.append(dot(ds_rim, q4))
            rim_value.append(dot(p_rim.astype(BF16), g4))
        own = pl.ds(s * 256, 256)
        qg[own, :] = (d_key + jnp.concatenate(rim_key, axis=0)).astype(BF16)
        kg[own, :] = (d_value + jnp.concatenate(rim_value, axis=0)).astype(BF16)
        if s == 0:
            station_sum.to_plane()
    signal = sig[...].reshape(512, 256)
    d_query, d_key, d_value = dq_w[...].reshape(512, 256), qg[...], kg[...]
    window_sum.put(0, dot(signal, d_query, "tn"))
    window_sum.put(1, dot(signal, d_key, "tn"))
    window_sum.put(2, dot(signal, d_value, "tn"))
    window_sum.to_core()
    signal_grad = (
        own_grads.astype(F32)
        + dot(d_query, wq[...], "nt")
        + dot(d_key, wk[...], "nt")
        + dot(d_value, wv[...], "nt")
    )
    sg_out[...] = signal_grad.astype(BF16).reshape(2, 256, 256)
    window_sum.to_plane()
    station_sum.to_line()
    window_sum.to_line()
    station_sum.back()
    window_sum.back()
    station_sum.pass_on()
    for copy in to_output:
        copy.wait_recv()
    bo_out[...] = bo[...]
    window_sum.pass_on()
    station_sum.finish()
    for copy in [*halos, *to_frames, *to_rows, *rims, *to_owner, *to_rims, *to_output]:
        copy.wait_send()
    fin_out[1536:4096, :] = station_sum.fin[...]
    window_sum.finish()
    fin_out[0:1536, :] = window_sum.fin[...]


def sum_scratch(count):
    dma = pltpu.SemaphoreType.DMA
    rows = count * 16
    return [
        pltpu.VMEM((count * 512, LANES), BF16),
        pltpu.VMEM((count * 256, LANES), BF16),
        pltpu.VMEM((count * 256, LANES), BF16),
        pltpu.VMEM((15, rows, LANES), BF16),
        pltpu.VMEM((8, rows, LANES), BF16),
        pltpu.VMEM((count * 512, LANES), BF16),
        dma((2,)), dma((15,)), dma((15,)), dma((7,)), dma((7,)),
        dma((15,)), dma((15,)), dma((16,)), dma((16,)),
    ]


def finish_kernel(factor, bo, sg, fin, o_bo, o_sg, *rest):
    outs, (wide, sem) = rest[:8], rest[8:]
    copies = [
        pltpu.make_async_copy(bo, o_bo, sem.at[8]),
        pltpu.make_async_copy(sg, o_sg, sem.at[9]),
    ]
    for copy in copies:
        copy.start()
    for i, ref in enumerate(outs):
        for j in range(2):
            wide[i, :, j * LANES : (j + 1) * LANES] = (
                fin[pl.ds((2 * i + j) * 256, 256), :].astype(F32) * factor
            )
        copies.append(pltpu.make_async_copy(wide.at[i], ref, sem.at[i]))
        copies[-1].start()
    for copy in copies:
        copy.wait()


def body(signal, cotangent, *rest):
    dma = pltpu.SemaphoreType.DMA
    vmem = pl.BlockSpec(memory_space=pltpu.VMEM)
    hbm = pl.BlockSpec(memory_space=pltpu.HBM)

    def b(*shape):
        return pltpu.VMEM(shape, BF16)

    def f(*shape):
        return pltpu.VMEM(shape, F32)

    words = pltpu.VMEM((16, 32), jnp.int32)
    scratch = [
        b(2, 256, 256), b(8, 256, 256), words, words,
        b(2, 512, 256), b(2, 512, 256), b(2, 512, 256), b(2, 512, 256), b(2, 512, 256),
        f(4, 2, 1, 512), f(2, 256, 512), f(2, 128, 512), f(2, 128, 512), f(4, 1, 512), f(4, 1, 512),
        f(4, 256, 512), f(4, 128, 512), f(4, 128, 512), b(2, 256, 256),
        b(32, 16, 256), b(32, 16, 256), f(128, 512), f(128, 512), b(512, 512), b(512, 512),
        b(512, 256), b(512, 256), b(512, 256), b(512, 256),
        b(512, 256), b(512, 256), b(512, 256), b(512, 256),
        b(32, 16, 256), b(32, 16, 256), b(2, 256, 256),
        b(2, 512, 256), b(2, 512, 256), f(4, 2, 1, 512), b(2, 256, 256),
        dma((12,)), dma((6,)), dma((6,)), dma((5, 15)), dma((5, 15)), dma((16,)), dma((16,)),
        *sum_scratch(5), *sum_scratch(3),
    ]
    *inputs, neighbours, neighbour_valid = (signal, cotangent, *rest)
    block_output, signal_grad, fin = pl.pallas_call(
        block_kernel,
        out_shape=[
            jax.ShapeDtypeStruct((2, 256, 256), BF16),
            jax.ShapeDtypeStruct((2, 256, 256), BF16),
            jax.ShapeDtypeStruct((4096, LANES), BF16),
        ],
        in_specs=[hbm] * 12,
        out_specs=[vmem] * 3,
        scratch_shapes=scratch,
        compiler_params=pltpu.CompilerParams(
            collective_id=0, has_side_effects=True, vmem_limit_bytes=48 * 1024 * 1024
        ),
        name="block",
    )(*inputs, neighbours.T, neighbour_valid.T)
    factor = 1.0 / math.sqrt(STN * 2 * TM * 256)
    order = pl.pallas_call(
        functools.partial(finish_kernel, factor),
        out_shape=[
            jax.ShapeDtypeStruct((2, 256, 256), BF16),
            jax.ShapeDtypeStruct((2, 256, 256), BF16),
        ]
        + [jax.ShapeDtypeStruct((256, 256), F32)] * 8,
        in_specs=[vmem] * 3,
        out_specs=[hbm] * 10,
        scratch_shapes=[f(8, 256, 256), dma((10,))],
        compiler_params=pltpu.CompilerParams(vmem_limit_bytes=8 * 1024 * 1024),
        name="finish",
    )(block_output, signal_grad, fin)
    bo, sg, wq, wk, wv, sq, sk, sv, so, wo = order
    return bo, sg, wq, wk, wv, wo, sq, sk, sv, so


def solution(mesh):
    return jax.shard_map(
        lambda *operands: tuple(body(*operands)),
        mesh=mesh,
        in_specs=(P("stn", "tm", None), P("stn", "tm", None), *([P()] * 10)),
        out_specs=(P("stn", "tm", None), P("stn", "tm", None), *([P()] * 8)),
        check_vma=False,
    )
```
